32 devices in a mesh: dp: 16 (over z, y, core), tensor: 2 (over x).
Axes of the slice: x: 2, y: 2, z: 4, core: 2. Of those that a mesh axis runs over, the one named last changes fastest.
Arguments:
- tokens: float32 [16384, 1024], P(('dp', 'tensor')), may hold values from -6 to 6
- norm_gain: float32 [1024], P(('dp', 'tensor')), may hold values from 0.5 to 1.5
- w_z: bfloat16 [1024, 2048], P('dp', 'tensor'), may hold values from -0.1875 to 0.1875
- w_x: bfloat16 [1024, 2048], P('dp', 'tensor'), may hold values from -0.1875 to 0.1875
- w_dt: bfloat16 [1024, 32], P('dp', 'tensor'), may hold values from -0.1875 to 0.1875
- w_bc: bfloat16 [1024, 256], P(('dp', 'tensor')), may hold values from -0.1875 to 0.1875
- w_out: bfloat16 [1024, 2048], P('dp', 'tensor'), may hold values from -0.125 to 0.125
- conv_x_w: float32 [2048, 4], P('tensor'), may hold values from -3 to 3
- conv_x_b: float32 [2048], P('tensor'), may hold values from -0.5 to 0.5
- conv_bc_w: float32 [256, 4], P(('dp', 'tensor')), may hold values from -3 to 3
- conv_bc_b: float32 [256], P(('dp', 'tensor')), may hold values from -0.5 to 0.5
- a_log: float32 [32], P('tensor'), may hold values from -1 to 1.5
- d_skip: float32 [32], P('tensor'), may hold values from 0.5 to 1.5
- dt_bias: float32 [32], P('tensor'), may hold values from -7 to -2.5
- norm_w: float32 [2048], P('tensor'), may hold values from 0.5 to 1.5
- block_seq: int32 [64], P('dp'), may hold values from 0 to 63, as said below
- block_len: int32 [64], P('dp'), may hold values from 0 to 256, as said below
- cotangent: float32 [16384, 1024], P(('dp', 'tensor')), may hold values from -6 to 6
Outputs:
- output: float32 [16384, 1024], P(('dp', 'tensor'))
- d_tokens: float32 [16384, 1024], P(('dp', 'tensor'))
- d_gain: float32 [1024], P(('dp', 'tensor'))
- d_w_z: float32 [1024, 2048], P('dp', 'tensor')
- d_w_x: float32 [1024, 2048], P('dp', 'tensor')
- d_w_dt: float32 [1024, 32], P('dp', 'tensor')
- d_w_bc: float32 [1024, 256], P(('dp', 'tensor'))
- d_w_out: float32 [1024, 2048], P('dp', 'tensor')
- d_conv_x_w: float32 [2048, 4], P('tensor')
- d_conv_x_b: float32 [2048], P('tensor')
- d_conv_bc_w: float32 [256, 4], P(('dp', 'tensor'))
- d_conv_bc_b: float32 [256], P(('dp', 'tensor'))
- d_a_log: float32 [32], P('tensor')
- d_d_skip: float32 [32], P('tensor')
- d_dt_bias: float32 [32], P('tensor')
- d_norm_w: float32 [2048], P('tensor')
The draws below stay inside these ranges and needn't reach their ends.
Inputs may be any that keep to these rules, and one draw needn't show every extreme that they name: `block_seq`: each index of dp holds 4 slots; a sequence takes consecutive slots of one index starting at a slot's first row, every slot but its last full; adjacent slots of one index carry the same value exactly when they hold one sequence; an empty slot has a value no other slot has. `block_len`: rows in use count from a slot's start; an empty slot has 0; fewer than 256 only in a sequence's last slot.
All inputs are finite; a program needn't handle non-finite values.
Results may differ from the reference program's by a relative error of at most 0.0082.
Values may be sent and summed in bfloat16 or wider, within the bound.
A program may use at most 192 MiB of HBM per device.

```python
import jax
import jax.numpy as jnp
from jax import lax

D = 1024
INNER = 2048
HEADS = 32
HEADDIM = 64
STATE = 128
CONV = 4
BLOCK = 256
SLOTS = 4
BLOCKS = 64
TOKENS = 16384
N_TENSOR = 2


def block_layout(key):
    base_key = jax.random.fold_in(key, 7)
    key_live, key_start, key_length = jax.random.split(base_key, 3)
    groups = BLOCKS // SLOTS
    live_counts = jax.random.randint(key_live, (groups,), SLOTS // 2, SLOTS + 1)
    live_counts = live_counts.at[0].set(SLOTS).at[1].set(SLOTS // 2)
    starts = jax.random.randint(key_start, (groups, SLOTS), 0, 2)
    starts = starts.at[:, 0].set(1)
    if SLOTS > 1:
        starts = starts.at[0, 1].set(0)
    starts = starts.at[groups - 1, SLOTS - 1].set(1)
    slot_index = jnp.arange(SLOTS)[None, :]
    live_mask = slot_index < live_counts[:, None]
    starts = jnp.where(live_mask, starts, 1)
    begin_slot = lax.cummax(jnp.where(starts == 1, slot_index, 0), axis=1)
    seq_ids = jnp.arange(groups)[:, None] * SLOTS + begin_slot
    following = jnp.concatenate([starts[:, 1:], jnp.ones((groups, 1), starts.dtype)], axis=1)
    partial_len = jax.random.randint(key_length, (groups, SLOTS), 1, BLOCK + 1)
    lengths = jnp.where(live_mask, jnp.where(following == 1, partial_len, BLOCK), 0)
    lengths = lengths.at[0, 0].set(BLOCK)
    return (seq_ids.reshape(-1).astype(jnp.int32), lengths.reshape(-1).astype(jnp.int32))


def draw_block_seq(key, part):
    return block_layout(key)[0]


def draw_block_len(key, part):
    return block_layout(key)[1]


def with_spikes(values, rng, source, target, parts, factor):
    def block_of(dim):
        return (jnp.arange(values.shape[dim]) // (values.shape[dim] // parts)).reshape((-1,) + (1,) * (values.ndim - 1 - dim))

    first = jax.random.permutation(rng, parts)[block_of(target)]
    second = (block_of(target) + parts // 2) % parts
    return jnp.where((block_of(source) == first) | (block_of(source) == second), factor * values, values)


def shard_levels(rng, extent, cuts, least, largest):
    def one(axis_at, shards_of):
        steps = jax.random.uniform(jax.random.fold_in(jax.random.fold_in(rng, 6), axis_at), (shards_of,), jnp.float32, least / len(cuts), largest / len(cuts))
        return jnp.repeat(jnp.exp(steps), extent[axis_at] // shards_of).reshape((-1,) + (1,) * (len(extent) - axis_at - 1))

    level = one(*cuts[0])
    for cut in cuts[1:]:
        level = level * one(*cut)
    return level


def noise(stream_key, shape, width, reach, shards=(), held_as=jnp.bfloat16):
    gain = shard_levels(stream_key, shape, shards, -0.22, 0.18) if shards else 1.0
    values = jax.random.normal(stream_key, shape, jnp.float32) * width * gain
    return jnp.minimum(jnp.maximum(values, -reach), reach).astype(held_as)


def noise_with(key, dims, deviation, reach, cuts, heavy, kind=jnp.bfloat16):
    values = deviation * jax.random.normal(key, dims, jnp.float32)
    if cuts:
        values = values * shard_levels(key, dims, cuts, -0.22, 0.18)
    return jnp.clip(with_spikes(values, jax.random.fold_in(key, 3), *heavy), -reach, reach).astype(kind)


def setup_inputs(seed: int = 0) -> dict:
    splits = jax.random.split(jax.random.key(seed), 19)
    tokens = noise_with(splits[0], (TOKENS, D), 1.0, 6.0, ((0, 32),), (0, 1, 32, 2.75), jnp.float32)
    norm_gain = jnp.clip(1.0 + 0.1 * jax.random.normal(splits[1], (D,), jnp.float32), 0.5, 1.5)
    w_z = noise(splits[2], (D, INNER), D ** -0.5, 0.1875, ((0, 16), (1, 2)))
    w_x = noise(splits[3], (D, INNER), D ** -0.5, 0.1875, ((0, 16), (1, 2)))
    w_dt = noise(splits[4], (D, HEADS), D ** -0.5, 0.1875, ((0, 16), (1, 2)))
    w_bc = noise(splits[5], (D, 2 * STATE), D ** -0.5, 0.1875, ((0, 32),))
    w_out = noise(splits[6], (D, INNER), INNER ** -0.5, 0.125, ((0, 16), (1, 2)))
    conv_x_w = noise(splits[7], (INNER, CONV), CONV ** -0.5, 3.0, ((0, 2),), jnp.float32)
    conv_x_b = jnp.clip(jax.random.uniform(splits[8], (INNER,), jnp.float32, -0.5, 0.5) * shard_levels(splits[8], (INNER,), ((0, 2),), -0.4, 0.0), -0.5, 0.5)
    conv_bc_w = noise(splits[9], (2 * STATE, CONV), CONV ** -0.5, 3.0, ((0, 32),), jnp.float32)
    conv_bc_b = jnp.clip(jax.random.uniform(splits[10], (2 * STATE,), jnp.float32, -0.5, 0.5) * shard_levels(splits[10], (2 * STATE,), ((0, 32),), -0.4, 0.0), -0.5, 0.5)
    a_log = jnp.clip(-1.0 + 2.5 * jax.random.uniform(splits[11], (HEADS,), jnp.float32) ** shard_levels(splits[11], (HEADS,), ((0, 2),), -0.2, 0.2), -1.0, 1.5)
    d_skip = jnp.clip(0.5 + 1.0 * jax.random.uniform(splits[12], (HEADS,), jnp.float32) ** shard_levels(splits[12], (HEADS,), ((0, 2),), -0.2, 0.2), 0.5, 1.5)
    dt_bias = jnp.clip(-7.0 + 4.5 * jax.random.uniform(splits[13], (HEADS,), jnp.float32) ** shard_levels(splits[13], (HEADS,), ((0, 2),), -0.2, 0.2), -7.0, -2.5)
    norm_w = jnp.clip(1.0 + 0.1 * jax.random.normal(splits[14], (INNER,), jnp.float32), 0.5, 1.5)
    block_seq = draw_block_seq(jax.random.fold_in(splits[18], 71), 0)
    block_len = draw_block_len(jax.random.fold_in(splits[18], 71), 0)
    cotangent = noise_with(splits[17], (TOKENS, D), 1.0, 6.0, ((0, 32),), (0, 1, 32, 2.75), jnp.float32)
    return {"tokens": tokens, "norm_gain": norm_gain, "w_z": w_z, "w_x": w_x, "w_dt": w_dt, "w_bc": w_bc, "w_out": w_out, "conv_x_w": conv_x_w, "conv_x_b": conv_x_b, "conv_bc_w": conv_bc_w, "conv_bc_b": conv_bc_b, "a_log": a_log, "d_skip": d_skip, "dt_bias": dt_bias, "norm_w": norm_w, "block_seq": block_seq, "block_len": block_len, "cotangent": cotangent}


EPSILON = 1e-05
HIGHEST_PREC = lax.Precision.HIGHEST

def shift_rows(values, lag_rows):
    if lag_rows == 0:
        return values
    zero_rows = jnp.zeros((lag_rows,) + values.shape[1:], values.dtype)
    return jnp.concatenate([zero_rows, values[:-lag_rows]], axis=0)

def causal_conv(values, weights, bias_vec, keep_masks):
    taps_count = weights.shape[1]
    summed = jnp.zeros_like(values) + bias_vec[None, :]
    for offset in range(taps_count):
        lag_rows = taps_count - 1 - offset
        shifted = shift_rows(values, lag_rows) * keep_masks[lag_rows][:, None]
        summed = summed + shifted * weights[:, offset][None, :]
    return jax.nn.silu(summed)

def scan_heads(x_pre, bc_pre, dt_raw, conv_x_w, conv_x_b, conv_bc_w, conv_bc_b, a_log, d_skip, dt_bias, carry_flags, token_mask):
    row_count = x_pre.shape[0]
    slot_count = row_count // BLOCK
    head_count = dt_raw.shape[1]
    position = jnp.arange(row_count) % BLOCK
    carry_rows = jnp.repeat(carry_flags, BLOCK)
    keep_masks = [jnp.where(position >= lag_rows, jnp.ones_like(carry_rows), carry_rows) for lag_rows in range(conv_x_w.shape[1])]
    x_conv = causal_conv(x_pre, conv_x_w, conv_x_b, keep_masks)
    bc_conv = causal_conv(bc_pre, conv_bc_w, conv_bc_b, keep_masks)
    state_in = bc_conv[:, :STATE].reshape(slot_count, BLOCK, STATE)
    state_out = bc_conv[:, STATE:].reshape(slot_count, BLOCK, STATE)
    inputs = x_conv.reshape(slot_count, BLOCK, head_count, HEADDIM)
    steps_dt = jax.nn.softplus(dt_raw + dt_bias[None, :]) * token_mask[:, None]
    decay_rates = (steps_dt * (-jnp.exp(a_log))[None, :]).reshape(slot_count, BLOCK, head_count)
    steps_three = steps_dt.reshape(slot_count, BLOCK, head_count)
    lower_mask = (jnp.arange(BLOCK)[:, None] >= jnp.arange(BLOCK)[None, :]).astype(x_pre.dtype)
    cumulative = jnp.einsum('ij,sjh->sih', lower_mask, decay_rates, precision=HIGHEST_PREC)
    scores_cb = jnp.einsum('sin,sjn->sij', state_out, state_in, precision=HIGHEST_PREC)
    differ = cumulative[:, :, None, :] - cumulative[:, None, :, :]
    decay_mat = jnp.exp(jnp.where(lower_mask[None, :, :, None] > 0.5, differ, -1e+30))
    mixing = scores_cb[:, :, :, None] * decay_mat * steps_three[:, None, :, :]
    y_local = jnp.einsum('sijh,sjhp->sihp', mixing, inputs, precision=HIGHEST_PREC)
    span_total = cumulative[:, -1, :]
    to_end = jnp.exp(span_total[:, None, :] - cumulative) * steps_three
    block_states = jnp.einsum('sjn,sjh,sjhp->shnp', state_in, to_end, inputs, precision=HIGHEST_PREC)
    carried = []
    current = jnp.zeros((head_count, STATE, HEADDIM), x_pre.dtype)
    for slot_index in range(slot_count):
        current = current * carry_flags[slot_index]
        carried.append(current)
        current = current * jnp.exp(span_total[slot_index])[:, None, None] + block_states[slot_index]
    entering = jnp.stack(carried)
    y_state = jnp.einsum('sin,shnp->sihp', state_out, entering, precision=HIGHEST_PREC) * jnp.exp(cumulative)[:, :, :, None]
    output = y_local + y_state + inputs * d_skip[None, None, :, None]
    return output.reshape(row_count, head_count * HEADDIM)

def reference(tokens, norm_gain, w_z, w_x, w_dt, w_bc, w_out, conv_x_w, conv_x_b, conv_bc_w, conv_bc_b, a_log, d_skip, dt_bias, norm_w, block_seq, block_len, cotangent):
    rows_blk = SLOTS * BLOCK
    group_heads = HEADS // N_TENSOR
    group_cols = group_heads * HEADDIM

    def one_block(grad_sums, block_data):
        tok_blk, cot_blk, seq_blk, len_blk = block_data
        slot_index = jnp.arange(SLOTS)
        previous = jnp.concatenate([seq_blk[:1] - 1, seq_blk[:-1]])
        carry_flags = ((slot_index > 0) & (seq_blk == previous)).astype(jnp.float32)
        token_mask = (jnp.arange(rows_blk) % BLOCK < jnp.repeat(len_blk, BLOCK)).astype(jnp.float32)
        mean_sq = lax.optimization_barrier(jnp.mean(tok_blk * tok_blk, axis=1, keepdims=True))
        inv_rms = lax.rsqrt(mean_sq + EPSILON)
        unit_rows = tok_blk * inv_rms
        normed = (unit_rows * norm_gain[None, :]).astype(jnp.bfloat16)
        gate_pre = jnp.dot(normed, w_z, preferred_element_type=jnp.float32)
        x_pre = jnp.dot(normed, w_x, preferred_element_type=jnp.float32)
        bc_pre = jnp.dot(normed, w_bc, preferred_element_type=jnp.float32)
        dt_raw = jnp.dot(normed, w_dt, preferred_element_type=jnp.float32)

        def local_scan(xp_in, bc_in, dt_in, cxw, cxb, cbw, cbb, alog_in, skip_in, bias_in):
            return scan_heads(xp_in, bc_in, dt_in, cxw, cxb, cbw, cbb, alog_in, skip_in, bias_in, carry_flags, token_mask)
        y_parts = []
        back_parts = []
        for group_index in range(N_TENSOR):
            col_lo = group_index * group_cols
            head_lo = group_index * group_heads
            y_group, back_group = jax.vjp(local_scan, x_pre[:, col_lo:col_lo + group_cols], bc_pre, dt_raw[:, head_lo:head_lo + group_heads], conv_x_w[col_lo:col_lo + group_cols], conv_x_b[col_lo:col_lo + group_cols], conv_bc_w, conv_bc_b, a_log[head_lo:head_lo + group_heads], d_skip[head_lo:head_lo + group_heads], dt_bias[head_lo:head_lo + group_heads])
            y_parts.append(y_group)
            back_parts.append(back_group)
        y_full = jnp.concatenate(y_parts, axis=1)
        gated_rows = y_full * jax.nn.silu(gate_pre)
        sq_sum = lax.optimization_barrier(jnp.sum(gated_rows * gated_rows, axis=1, keepdims=True))
        inv_g = lax.rsqrt(sq_sum / INNER + EPSILON)
        unit_g = gated_rows * inv_g
        hidden = (unit_g * norm_w[None, :] * token_mask[:, None]).astype(jnp.bfloat16)
        branch = jnp.dot(hidden, w_out.T, preferred_element_type=jnp.float32)
        out_blk = tok_blk + branch
        cot_b = cot_blk.astype(jnp.bfloat16)
        d_hidden = jnp.dot(cot_b, w_out, preferred_element_type=jnp.float32)
        g_w_out = jnp.dot(cot_b.T, hidden, preferred_element_type=jnp.float32)
        d_unit = d_hidden * norm_w[None, :] * token_mask[:, None]
        g_norm_w = lax.optimization_barrier(jnp.sum(d_hidden * unit_g * token_mask[:, None], axis=0))
        inner_sum = lax.optimization_barrier(jnp.sum(d_unit * unit_g, axis=1, keepdims=True))
        d_gated = inv_g * (d_unit - unit_g * inner_sum / INNER)
        sigmoid_gate = jax.nn.sigmoid(gate_pre)
        d_y = d_gated * gate_pre * sigmoid_gate
        d_gate = d_gated * y_full * sigmoid_gate * (1.0 + gate_pre * (1.0 - sigmoid_gate))
        xg_parts, dtg_parts, cxw_parts, cxb_parts, alog_parts, skip_parts, bias_parts = ([], [], [], [], [], [], [])
        g_cbw = jnp.zeros_like(conv_bc_w)
        g_cbb = jnp.zeros_like(conv_bc_b)
        g_w_bc = jnp.zeros((D, 2 * STATE), jnp.float32)
        d_normed = jnp.zeros((rows_blk, D), jnp.float32)
        for group_index in range(N_TENSOR):
            col_lo = group_index * group_cols
            pieces = back_parts[group_index](d_y[:, col_lo:col_lo + group_cols])
            xg_parts.append(pieces[0])
            dtg_parts.append(pieces[2])
            cxw_parts.append(pieces[3])
            cxb_parts.append(pieces[4])
            g_cbw = g_cbw + pieces[5]
            g_cbb = g_cbb + pieces[6]
            alog_parts.append(pieces[7])
            skip_parts.append(pieces[8])
            bias_parts.append(pieces[9])
            bc_g = pieces[1].astype(jnp.bfloat16)
            g_w_bc = g_w_bc + jnp.dot(normed.T, bc_g, preferred_element_type=jnp.float32)
            d_normed = d_normed + jnp.dot(bc_g, w_bc.T, preferred_element_type=jnp.float32)
        gate_g = d_gate.astype(jnp.bfloat16)
        x_g = jnp.concatenate(xg_parts, axis=1).astype(jnp.bfloat16)
        dt_g = jnp.concatenate(dtg_parts, axis=1).astype(jnp.bfloat16)
        g_w_z = jnp.dot(normed.T, gate_g, preferred_element_type=jnp.float32)
        g_w_x = jnp.dot(normed.T, x_g, preferred_element_type=jnp.float32)
        g_w_dt = jnp.dot(normed.T, dt_g, preferred_element_type=jnp.float32)
        d_normed = d_normed + jnp.dot(gate_g, w_z.T, preferred_element_type=jnp.float32)
        d_normed = d_normed + jnp.dot(x_g, w_x.T, preferred_element_type=jnp.float32)
        d_normed = d_normed + jnp.dot(dt_g, w_dt.T, preferred_element_type=jnp.float32)
        g_gain = lax.optimization_barrier(jnp.sum(d_normed * unit_rows, axis=0))
        d_unit_r = d_normed * norm_gain[None, :]
        d_tok = cot_blk + inv_rms * (d_unit_r - unit_rows * lax.optimization_barrier(jnp.mean(d_unit_r * unit_rows, axis=1, keepdims=True)))
        block_grads = (g_gain, g_w_z, g_w_x, g_w_dt, g_w_bc, g_w_out, jnp.concatenate(cxw_parts, axis=0), jnp.concatenate(cxb_parts, axis=0), g_cbw, g_cbb, jnp.concatenate(alog_parts), jnp.concatenate(skip_parts), jnp.concatenate(bias_parts), g_norm_w)
        new_sums = tuple((old + new for old, new in zip(grad_sums, block_grads)))
        return (new_sums, (out_blk, d_tok))
    init_sums = (jnp.zeros((D,), jnp.float32), jnp.zeros((D, INNER), jnp.float32), jnp.zeros((D, INNER), jnp.float32), jnp.zeros((D, HEADS), jnp.float32), jnp.zeros((D, 2 * STATE), jnp.float32), jnp.zeros((D, INNER), jnp.float32), jnp.zeros((INNER, CONV), jnp.float32), jnp.zeros((INNER,), jnp.float32), jnp.zeros((2 * STATE, CONV), jnp.float32), jnp.zeros((2 * STATE,), jnp.float32), jnp.zeros((HEADS,), jnp.float32), jnp.zeros((HEADS,), jnp.float32), jnp.zeros((HEADS,), jnp.float32), jnp.zeros((INNER,), jnp.float32))
    groups = tokens.shape[0] // rows_blk
    grad_sums, (out_rows, dtok_rows) = lax.scan(one_block, init_sums, (tokens.reshape(groups, rows_blk, D), cotangent.reshape(groups, rows_blk, D), block_seq.reshape(groups, SLOTS), block_len.reshape(groups, SLOTS)))
    g_gain, g_w_z, g_w_x, g_w_dt, g_w_bc, g_w_out, g_cxw, g_cxb, g_cbw, g_cbb, g_alog, g_skip, g_bias, g_norm_w = grad_sums
    return (out_rows.reshape(tokens.shape), dtok_rows.reshape(tokens.shape), g_gain, g_w_z, g_w_x, g_w_dt, g_w_bc, g_w_out, g_cxw, g_cxb, g_cbw, g_cbb, g_alog, g_skip, g_bias, g_norm_w)
```

```python
import jax
import jax.numpy as jnp
from jax import lax
from jax.sharding import PartitionSpec as P

INNER = 2048
HEADDIM = 64
STATE = 128
BLOCK = 256


EPSILON = 1e-05
HIGHEST_PREC = lax.Precision.HIGHEST
HIGH_PREC = lax.Precision.HIGH


def shift_rows(values, lag_rows):
    if lag_rows == 0:
        return values
    zero_rows = jnp.zeros((lag_rows,) + values.shape[1:], values.dtype)
    return jnp.concatenate([zero_rows, values[:-lag_rows]], axis=0)


def causal_conv(values, weights, bias_vec, keep_masks):
    taps_count = weights.shape[1]
    summed = jnp.zeros_like(values) + bias_vec[None, :]
    for offset in range(taps_count):
        lag_rows = taps_count - 1 - offset
        shifted = shift_rows(values, lag_rows) * keep_masks[lag_rows][:, None]
        summed = summed + shifted * weights[:, offset][None, :]
    return jax.nn.silu(summed)


def scan_heads(
    x_pre,
    bc_pre,
    dt_raw,
    conv_x_w,
    conv_x_b,
    conv_bc_w,
    conv_bc_b,
    a_log,
    d_skip,
    dt_bias,
    carry_flags,
    token_mask,
):
    row_count = x_pre.shape[0]
    slot_count = row_count // BLOCK
    head_count = dt_raw.shape[1]
    position = jnp.arange(row_count) % BLOCK
    carry_rows = jnp.repeat(carry_flags, BLOCK)
    keep_masks = [
        jnp.where(position >= lag_rows, jnp.ones_like(carry_rows), carry_rows)
        for lag_rows in range(conv_x_w.shape[1])
    ]
    x_conv = causal_conv(x_pre, conv_x_w, conv_x_b, keep_masks)
    bc_conv = causal_conv(bc_pre, conv_bc_w, conv_bc_b, keep_masks)
    state_in = bc_conv[:, :STATE].reshape(slot_count, BLOCK, STATE)
    state_out = bc_conv[:, STATE:].reshape(slot_count, BLOCK, STATE)
    inputs = x_conv.reshape(slot_count, BLOCK, head_count, HEADDIM)
    steps_dt = jax.nn.softplus(dt_raw + dt_bias[None, :]) * token_mask[:, None]
    decay_rates = (steps_dt * (-jnp.exp(a_log))[None, :]).reshape(slot_count, BLOCK, head_count)
    steps_three = steps_dt.reshape(slot_count, BLOCK, head_count)
    lower_mask = (jnp.arange(BLOCK)[:, None] >= jnp.arange(BLOCK)[None, :]).astype(x_pre.dtype)
    cumulative = jnp.einsum("ij,sjh->sih", lower_mask, decay_rates, precision=HIGHEST_PREC)
    scores_cb = jnp.einsum("sin,sjn->sij", state_out, state_in, precision=HIGH_PREC)
    differ = cumulative[:, :, None, :] - cumulative[:, None, :, :]
    decay_mat = jnp.exp(jnp.where(lower_mask[None, :, :, None] > 0.5, differ, -1e30))
    mixing = scores_cb[:, :, :, None] * decay_mat * steps_three[:, None, :, :]
    y_local = jnp.einsum("sijh,sjhp->sihp", mixing, inputs, precision=HIGH_PREC)
    span_total = cumulative[:, -1, :]
    to_end = jnp.exp(span_total[:, None, :] - cumulative) * steps_three
    block_states = jnp.einsum(
        "sjn,sjh,sjhp->shnp", state_in, to_end, inputs, precision=HIGH_PREC
    )
    carried = []
    current = jnp.zeros((head_count, STATE, HEADDIM), x_pre.dtype)
    for slot_index in range(slot_count):
        current = current * carry_flags[slot_index]
        carried.append(current)
        current = (
            current * jnp.exp(span_total[slot_index])[:, None, None] + block_states[slot_index]
        )
    entering = jnp.stack(carried)
    y_state = (
        jnp.einsum("sin,shnp->sihp", state_out, entering, precision=HIGH_PREC)
        * jnp.exp(cumulative)[:, :, :, None]
    )
    output = y_local + y_state + inputs * d_skip[None, None, :, None]
    return output.reshape(row_count, head_count * HEADDIM)


def dot_nt(left, right):
    return lax.dot_general(
        left, right, (((1,), (1,)), ((), ())), preferred_element_type=jnp.float32
    )


def dot_tn(left, right):
    return lax.dot_general(
        left, right, (((0,), (0,)), ((), ())), preferred_element_type=jnp.float32
    )


def tensor_scatter_sum(parts):
    size = parts.shape[0]
    own = lax.axis_index("tensor")
    total = lax.dynamic_index_in_dim(parts, own, 0, keepdims=False)
    for step in range(1, size):
        outgoing = lax.dynamic_index_in_dim(parts, (own + step) % size, 0, keepdims=False)
        ring = [(source, (source + step) % size) for source in range(size)]
        total = total + lax.ppermute(outgoing, "tensor", ring)
    return total


def scatter_dp(values):
    return lax.psum_scatter(
        values.astype(jnp.bfloat16), "dp", scatter_dimension=0, tiled=True
    ).astype(jnp.float32)


def per_device(
    tokens,
    norm_gain,
    w_z,
    w_x,
    w_dt,
    w_bc,
    w_out,
    conv_x_w,
    conv_x_b,
    conv_bc_w,
    conv_bc_b,
    a_log,
    d_skip,
    dt_bias,
    norm_w,
    block_seq,
    block_len,
    cotangent,
):
    dp_size = lax.axis_size("dp")
    tensor_size = lax.axis_size("tensor")
    bc_rows, bc_width = w_bc.shape
    width_local = w_z.shape[1]
    weight_rows = w_z.shape[0]
    bc_flat = w_bc.reshape(weight_rows, bc_width * bc_rows // weight_rows)
    bc_cols = bc_flat.shape[1]
    packed = lax.all_gather(
        jnp.concatenate([w_z, w_x, bc_flat, w_dt], axis=1), "dp", axis=0, tiled=True
    )
    z_full = packed[:, :width_local]
    x_full = packed[:, width_local : 2 * width_local]
    bc_own = packed[:, 2 * width_local : 2 * width_local + bc_cols]
    dt_full = packed[:, 2 * width_local + bc_cols :]

    gain_len, conv_len, taps = norm_gain.shape[0], conv_bc_w.shape[0], conv_bc_w.shape[1]
    small = jnp.concatenate([norm_gain, conv_bc_w.reshape(-1), conv_bc_b])
    small_full = lax.all_gather(small, ("dp", "tensor"), axis=0, tiled=False)
    gain_full = small_full[:, :gain_len].reshape(-1)
    conv_bcw_full = small_full[:, gain_len : gain_len + conv_len * taps].reshape(-1, taps)
    conv_bcb_full = small_full[:, gain_len + conv_len * taps :].reshape(-1)

    mean_sq = jnp.mean(tokens * tokens, axis=1, keepdims=True)
    inv_rms = lax.rsqrt(mean_sq + EPSILON)
    unit_rows = tokens * inv_rms
    normed_own = (unit_rows * gain_full[None, :]).astype(jnp.bfloat16)
    own_rows = normed_own.shape[0]
    bc_extra = bc_own.reshape(-1, normed_own.shape[1])
    joined_rows = lax.all_gather(
        jnp.concatenate([normed_own, bc_extra], axis=0), "tensor", axis=0, tiled=False
    )
    normed = joined_rows[:, :own_rows].reshape(-1, normed_own.shape[1])
    bc_pair = joined_rows[:, own_rows:].reshape(tensor_size, dp_size, bc_rows, bc_width)
    bc_weight = bc_pair.transpose(1, 0, 2, 3).reshape(-1, bc_width)
    cot_in, w_out_in, normed = lax.optimization_barrier(
        (cotangent.astype(jnp.bfloat16), w_out, normed)
    )
    cot_rows = lax.all_gather(cot_in, "tensor", axis=0, tiled=True)
    out_full = lax.all_gather(w_out_in, "dp", axis=0, tiled=True)
    row_count = normed.shape[0]
    slot_count = block_seq.shape[0]
    slot_index = jnp.arange(slot_count)
    previous = jnp.concatenate([block_seq[:1] - 1, block_seq[:-1]])
    carry_flags = ((slot_index > 0) & (block_seq == previous)).astype(jnp.float32)
    token_mask = (jnp.arange(row_count) % BLOCK < jnp.repeat(block_len, BLOCK)).astype(jnp.float32)
    gate_pre = jnp.dot(normed, z_full, preferred_element_type=jnp.float32)
    x_pre = jnp.dot(normed, x_full, preferred_element_type=jnp.float32)
    bc_pre = jnp.dot(normed, bc_weight, preferred_element_type=jnp.float32)
    dt_raw = jnp.dot(normed, dt_full, preferred_element_type=jnp.float32)

    def local_scan(xp_in, bc_in, dt_in, cxw, cxb, cbw, cbb, alog_in, skip_in, bias_in):
        return scan_heads(
            xp_in,
            bc_in,
            dt_in,
            cxw,
            cxb,
            cbw,
            cbb,
            alog_in,
            skip_in,
            bias_in,
            carry_flags,
            token_mask,
        )

    y_local, scan_back = jax.vjp(
        local_scan,
        x_pre,
        bc_pre,
        dt_raw,
        conv_x_w,
        conv_x_b,
        conv_bcw_full,
        conv_bcb_full,
        a_log,
        d_skip,
        dt_bias,
    )
    gated_rows = y_local * jax.nn.silu(gate_pre)
    sq_sum = lax.psum(jnp.sum(gated_rows * gated_rows, axis=1), "tensor")
    inv_g = lax.rsqrt(sq_sum[:, None] / INNER + EPSILON)
    unit_g = gated_rows * inv_g
    hidden = (unit_g * norm_w[None, :] * token_mask[:, None]).astype(jnp.bfloat16)
    d_hidden = jnp.dot(cot_rows, out_full, preferred_element_type=jnp.float32)
    g_w_out_part = dot_tn(cot_rows, hidden).astype(jnp.bfloat16)
    branch_part = dot_nt(hidden, out_full).astype(jnp.bfloat16)
    d_unit = d_hidden * norm_w[None, :] * token_mask[:, None]
    g_norm_w = jnp.sum(d_hidden * unit_g * token_mask[:, None], axis=0)
    inner_sum = lax.psum(jnp.sum(d_unit * unit_g, axis=1), "tensor")
    d_gated = inv_g * (d_unit - unit_g * inner_sum[:, None] / INNER)
    sigmoid_gate = jax.nn.sigmoid(gate_pre)
    d_y = d_gated * gate_pre * sigmoid_gate
    d_gate = d_gated * y_local * sigmoid_gate * (1.0 + gate_pre * (1.0 - sigmoid_gate))
    gate_g = d_gate.astype(jnp.bfloat16)
    g_w_z_part = dot_tn(normed, gate_g).astype(jnp.bfloat16)
    d_y, g_w_out_part, branch_part, g_w_z_part = lax.optimization_barrier(
        (d_y, g_w_out_part, branch_part, g_w_z_part)
    )
    g_w_out = scatter_dp(g_w_out_part)
    g_w_z = scatter_dp(g_w_z_part)
    branch = lax.psum_scatter(branch_part, "tensor", scatter_dimension=0, tiled=True)
    output = tokens + branch.astype(jnp.float32)
    d_xp, d_bc, d_dt, g_cxw, g_cxb, g_cbw, g_cbb, g_alog, g_skip, g_bias = scan_back(d_y)
    x_g = d_xp.astype(jnp.bfloat16)
    dt_g = d_dt.astype(jnp.bfloat16)
    bc_g = d_bc.astype(jnp.bfloat16)
    d_normed_part = dot_nt(gate_g, z_full) + dot_nt(x_g, x_full)
    d_normed_part = d_normed_part + dot_nt(dt_g, dt_full) + dot_nt(bc_g, bc_weight)
    joined = jnp.concatenate([x_g, bc_g, dt_g], axis=1)
    in_grads = scatter_dp(dot_tn(normed, joined))
    g_w_x = in_grads[:, :width_local]
    g_bc_rows = in_grads[:, width_local : width_local + bc_width]
    g_w_dt = in_grads[:, width_local + bc_width :]
    d_normed = lax.psum_scatter(
        d_normed_part.astype(jnp.bfloat16), "tensor", scatter_dimension=0, tiled=True
    ).astype(jnp.float32)
    d_unit_r = d_normed * gain_full[None, :]
    d_tokens = cotangent + inv_rms * (
        d_unit_r - unit_rows * jnp.mean(d_unit_r * unit_rows, axis=1, keepdims=True)
    )

    group_parts = (g_cxw, g_cxb, g_alog, g_skip, g_bias, g_norm_w, g_cbw, g_cbb)
    flat = lax.psum(jnp.concatenate([part.reshape(-1) for part in group_parts]), "dp")
    pieces = []
    offset = 0
    for part in group_parts:
        pieces.append(flat[offset : offset + part.size].reshape(part.shape))
        offset += part.size
    g_cxw, g_cxb, g_alog, g_skip, g_bias, g_norm_w, g_cbw, g_cbb = pieces

    dp_index = lax.axis_index("dp")
    bc_here = lax.dynamic_slice_in_dim(bc_weight, dp_index * weight_rows, weight_rows, 0)
    gain_rows = (
        jnp.sum(g_w_z * w_z.astype(jnp.float32), axis=1)
        + jnp.sum(g_w_x * w_x.astype(jnp.float32), axis=1)
        + jnp.sum(g_w_dt * w_dt.astype(jnp.float32), axis=1)
        + jnp.sum(g_bc_rows * bc_here.astype(jnp.float32), axis=1)
    )
    conv_here = tensor_size * conv_len
    cbw_here = lax.dynamic_slice_in_dim(g_cbw, dp_index * conv_here, conv_here, 0)
    cbb_here = lax.dynamic_slice_in_dim(g_cbb, dp_index * conv_here, conv_here, 0)
    g_w_bc = tensor_scatter_sum(g_bc_rows.reshape(tensor_size, bc_rows, bc_width))
    shared = tensor_scatter_sum(
        jnp.concatenate(
            [
                gain_rows.reshape(tensor_size, gain_len),
                cbw_here.reshape(tensor_size, conv_len * taps),
                cbb_here.reshape(tensor_size, conv_len),
            ],
            axis=1,
        )
    )
    g_gain = shared[:gain_len] / norm_gain
    g_conv_bcw = shared[gain_len : gain_len + conv_len * taps].reshape(conv_len, taps)
    g_conv_bcb = shared[gain_len + conv_len * taps :]
    return (
        output,
        d_tokens,
        g_gain,
        g_w_z,
        g_w_x,
        g_w_dt,
        g_w_bc,
        g_w_out,
        g_cxw,
        g_cxb,
        g_conv_bcw,
        g_conv_bcb,
        g_alog,
        g_skip,
        g_bias,
        g_norm_w,
    )


def solution(mesh):
    return jax.shard_map(
        per_device,
        mesh=mesh,
        in_specs=(
            P(("dp", "tensor"), None),
            P(("dp", "tensor")),
            P("dp", "tensor"),
            P("dp", "tensor"),
            P("dp", "tensor"),
            P(("dp", "tensor"), None),
            P("dp", "tensor"),
            P("tensor", None),
            P("tensor"),
            P(("dp", "tensor"), None),
            P(("dp", "tensor")),
            P("tensor"),
            P("tensor"),
            P("tensor"),
            P("tensor"),
            P("dp"),
            P("dp"),
            P(("dp", "tensor"), None),
        ),
        out_specs=(
            P(("dp", "tensor"), None),
            P(("dp", "tensor"), None),
            P(("dp", "tensor")),
            P("dp", "tensor"),
            P("dp", "tensor"),
            P("dp", "tensor"),
            P(("dp", "tensor"), None),
            P("dp", "tensor"),
            P("tensor", None),
            P("tensor"),
            P(("dp", "tensor"), None),
            P(("dp", "tensor")),
            P("tensor"),
            P("tensor"),
            P("tensor"),
            P("tensor"),
        ),
        check_vma=False,
    )
```

```python
import jax
import jax.numpy as jnp
from jax import lax
from jax.sharding import PartitionSpec as P

INNER = 2048
HEADDIM = 64
STATE = 128
BLOCK = 256


EPSILON = 1e-05
HIGHEST_PREC = lax.Precision.HIGHEST
HIGH_PREC = lax.Precision.HIGH


def shift_rows(values, lag_rows):
    if lag_rows == 0:
        return values
    zero_rows = jnp.zeros((lag_rows,) + values.shape[1:], values.dtype)
    return jnp.concatenate([zero_rows, values[:-lag_rows]], axis=0)


def causal_conv(values, weights, bias_vec, keep_masks):
    taps_count = weights.shape[1]
    summed = jnp.zeros_like(values) + bias_vec[None, :]
    for offset in range(taps_count):
        lag_rows = taps_count - 1 - offset
        shifted = shift_rows(values, lag_rows) * keep_masks[lag_rows][:, None]
        summed = summed + shifted * weights[:, offset][None, :]
    return jax.nn.silu(summed)


def scan_heads(
    x_pre,
    bc_pre,
    dt_raw,
    conv_x_w,
    conv_x_b,
    conv_bc_w,
    conv_bc_b,
    a_log,
    d_skip,
    dt_bias,
    carry_flags,
    token_mask,
):
    row_count = x_pre.shape[0]
    slot_count = row_count // BLOCK
    head_count = dt_raw.shape[1]
    position = jnp.arange(row_count) % BLOCK
    carry_rows = jnp.repeat(carry_flags, BLOCK)
    keep_masks = [
        jnp.where(position >= lag_rows, jnp.ones_like(carry_rows), carry_rows)
        for lag_rows in range(conv_x_w.shape[1])
    ]
    x_conv = causal_conv(x_pre, conv_x_w, conv_x_b, keep_masks)
    bc_conv = causal_conv(bc_pre, conv_bc_w, conv_bc_b, keep_masks)
    state_in = bc_conv[:, :STATE].reshape(slot_count, BLOCK, STATE)
    state_out = bc_conv[:, STATE:].reshape(slot_count, BLOCK, STATE)
    inputs = x_conv.reshape(slot_count, BLOCK, head_count, HEADDIM)
    steps_dt = jax.nn.softplus(dt_raw + dt_bias[None, :]) * token_mask[:, None]
    decay_rates = (steps_dt * (-jnp.exp(a_log))[None, :]).reshape(slot_count, BLOCK, head_count)
    steps_three = steps_dt.reshape(slot_count, BLOCK, head_count)
    lower_mask = (jnp.arange(BLOCK)[:, None] >= jnp.arange(BLOCK)[None, :]).astype(x_pre.dtype)
    cumulative = jnp.einsum("ij,sjh->sih", lower_mask, decay_rates, precision=HIGHEST_PREC)
    scores_cb = jnp.einsum("sin,sjn->sij", state_out, state_in, precision=HIGH_PREC)
    differ = cumulative[:, :, None, :] - cumulative[:, None, :, :]
    decay_mat = jnp.exp(jnp.where(lower_mask[None, :, :, None] > 0.5, differ, -1e30))
    mixing = scores_cb[:, :, :, None] * decay_mat * steps_three[:, None, :, :]
    y_local = jnp.einsum("sijh,sjhp->sihp", mixing, inputs, precision=HIGH_PREC)
    span_total = cumulative[:, -1, :]
    to_end = jnp.exp(span_total[:, None, :] - cumulative) * steps_three
    block_states = jnp.einsum(
        "sjn,sjh,sjhp->shnp", state_in, to_end, inputs, precision=HIGH_PREC
    )
    carried = []
    current = jnp.zeros((head_count, STATE, HEADDIM), x_pre.dtype)
    for slot_index in range(slot_count):
        current = current * carry_flags[slot_index]
        carried.append(current)
        current = (
            current * jnp.exp(span_total[slot_index])[:, None, None] + block_states[slot_index]
        )
    entering = jnp.stack(carried)
    y_state = (
        jnp.einsum("sin,shnp->sihp", state_out, entering, precision=HIGH_PREC)
        * jnp.exp(cumulative)[:, :, :, None]
    )
    output = y_local + y_state + inputs * d_skip[None, None, :, None]
    return output.reshape(row_count, head_count * HEADDIM)


def dot_nt(left, right):
    return lax.dot_general(
        left, right, (((1,), (1,)), ((), ())), preferred_element_type=jnp.float32
    )


def dot_tn(left, right):
    return lax.dot_general(
        left, right, (((0,), (0,)), ((), ())), preferred_element_type=jnp.float32
    )


def tensor_gather(piece):
    size = lax.axis_size("tensor")
    own = lax.axis_index("tensor")
    stacked = jnp.zeros((size,) + piece.shape, piece.dtype)
    stacked = lax.dynamic_update_index_in_dim(stacked, piece, own, 0)
    for step in range(1, size):
        ring = [(source, (source + step) % size) for source in range(size)]
        arrived = lax.ppermute(piece, "tensor", ring)
        stacked = lax.dynamic_update_index_in_dim(stacked, arrived, (own - step) % size, 0)
    return stacked


def tensor_scatter_rows(values):
    size = lax.axis_size("tensor")
    own = lax.axis_index("tensor")
    rows = values.shape[0] // size
    total = lax.dynamic_slice_in_dim(values, own * rows, rows, 0).astype(jnp.float32)
    for step in range(1, size):
        outgoing = lax.dynamic_slice_in_dim(values, (own + step) % size * rows, rows, 0)
        ring = [(source, (source + step) % size) for source in range(size)]
        arrived = lax.ppermute(outgoing.astype(jnp.bfloat16), "tensor", ring)
        total = total + arrived.astype(jnp.float32)
    return total


def tensor_scatter_sum(parts):
    size = parts.shape[0]
    own = lax.axis_index("tensor")
    total = lax.dynamic_index_in_dim(parts, own, 0, keepdims=False)
    for step in range(1, size):
        outgoing = lax.dynamic_index_in_dim(parts, (own + step) % size, 0, keepdims=False)
        ring = [(source, (source + step) % size) for source in range(size)]
        total = total + lax.ppermute(outgoing, "tensor", ring)
    return total


def scatter_dp(values):
    return lax.psum_scatter(
        values.astype(jnp.bfloat16), "dp", scatter_dimension=0, tiled=True
    ).astype(jnp.float32)


def per_device(
    tokens,
    norm_gain,
    w_z,
    w_x,
    w_dt,
    w_bc,
    w_out,
    conv_x_w,
    conv_x_b,
    conv_bc_w,
    conv_bc_b,
    a_log,
    d_skip,
    dt_bias,
    norm_w,
    block_seq,
    block_len,
    cotangent,
):
    dp_size = lax.axis_size("dp")
    tensor_size = lax.axis_size("tensor")
    bc_rows, bc_width = w_bc.shape
    width_local = w_z.shape[1]
    weight_rows = w_z.shape[0]
    bc_flat = w_bc.reshape(weight_rows, bc_width * bc_rows // weight_rows)
    bc_cols = bc_flat.shape[1]
    packed = lax.all_gather(
        jnp.concatenate([w_z, w_x, bc_flat, w_dt], axis=1), "dp", axis=0, tiled=True
    )
    z_full = packed[:, :width_local]
    x_full = packed[:, width_local : 2 * width_local]
    bc_own = packed[:, 2 * width_local : 2 * width_local + bc_cols]
    dt_full = packed[:, 2 * width_local + bc_cols :]

    gain_len, conv_len, taps = norm_gain.shape[0], conv_bc_w.shape[0], conv_bc_w.shape[1]
    small = jnp.concatenate([norm_gain, conv_bc_w.reshape(-1), conv_bc_b])
    small_full = lax.all_gather(small, ("dp", "tensor"), axis=0, tiled=False)
    gain_full = small_full[:, :gain_len].reshape(-1)
    conv_bcw_full = small_full[:, gain_len : gain_len + conv_len * taps].reshape(-1, taps)
    conv_bcb_full = small_full[:, gain_len + conv_len * taps :].reshape(-1)

    mean_sq = jnp.mean(tokens * tokens, axis=1, keepdims=True)
    inv_rms = lax.rsqrt(mean_sq + EPSILON)
    unit_rows = tokens * inv_rms
    normed_own = (unit_rows * gain_full[None, :]).astype(jnp.bfloat16)
    normed = tensor_gather(normed_own).reshape(-1, normed_own.shape[1])
    bc_pair = tensor_gather(bc_own.reshape(dp_size, bc_rows, bc_width))
    bc_weight = bc_pair.transpose(1, 0, 2, 3).reshape(-1, bc_width)
    cot_rows = tensor_gather(cotangent.astype(jnp.bfloat16)).reshape(normed.shape)
    w_out_in, _ = lax.optimization_barrier((w_out, packed))
    out_full = lax.all_gather(w_out_in, "dp", axis=0, tiled=True)
    row_count = normed.shape[0]
    slot_count = block_seq.shape[0]
    slot_index = jnp.arange(slot_count)
    previous = jnp.concatenate([block_seq[:1] - 1, block_seq[:-1]])
    carry_flags = ((slot_index > 0) & (block_seq == previous)).astype(jnp.float32)
    token_mask = (jnp.arange(row_count) % BLOCK < jnp.repeat(block_len, BLOCK)).astype(jnp.float32)
    gate_pre = jnp.dot(normed, z_full, preferred_element_type=jnp.float32)
    x_pre = jnp.dot(normed, x_full, preferred_element_type=jnp.float32)
    bc_pre = jnp.dot(normed, bc_weight, preferred_element_type=jnp.float32)
    dt_raw = jnp.dot(normed, dt_full, preferred_element_type=jnp.float32)

    def local_scan(xp_in, bc_in, dt_in, cxw, cxb, cbw, cbb, alog_in, skip_in, bias_in):
        return scan_heads(
            xp_in,
            bc_in,
            dt_in,
            cxw,
            cxb,
            cbw,
            cbb,
            alog_in,
            skip_in,
            bias_in,
            carry_flags,
            token_mask,
        )

    y_local, scan_back = jax.vjp(
        local_scan,
        x_pre,
        bc_pre,
        dt_raw,
        conv_x_w,
        conv_x_b,
        conv_bcw_full,
        conv_bcb_full,
        a_log,
        d_skip,
        dt_bias,
    )
    gated_rows = y_local * jax.nn.silu(gate_pre)
    sq_sum = lax.psum(jnp.sum(gated_rows * gated_rows, axis=1), "tensor")
    inv_g = lax.rsqrt(sq_sum[:, None] / INNER + EPSILON)
    unit_g = gated_rows * inv_g
    hidden = (unit_g * norm_w[None, :] * token_mask[:, None]).astype(jnp.bfloat16)
    d_hidden = jnp.dot(cot_rows, out_full, preferred_element_type=jnp.float32)
    g_w_out_part = dot_tn(cot_rows, hidden).astype(jnp.bfloat16)
    branch_part = dot_nt(hidden, out_full).astype(jnp.bfloat16)
    d_unit = d_hidden * norm_w[None, :] * token_mask[:, None]
    g_norm_w = jnp.sum(d_hidden * unit_g * token_mask[:, None], axis=0)
    inner_sum = lax.psum(jnp.sum(d_unit * unit_g, axis=1), "tensor")
    d_gated = inv_g * (d_unit - unit_g * inner_sum[:, None] / INNER)
    sigmoid_gate = jax.nn.sigmoid(gate_pre)
    d_y = d_gated * gate_pre * sigmoid_gate
    d_gate = d_gated * y_local * sigmoid_gate * (1.0 + gate_pre * (1.0 - sigmoid_gate))
    gate_g = d_gate.astype(jnp.bfloat16)
    g_w_z_part = dot_tn(normed, gate_g).astype(jnp.bfloat16)
    d_y, g_w_out_part, branch_part, g_w_z_part = lax.optimization_barrier(
        (d_y, g_w_out_part, branch_part, g_w_z_part)
    )
    early_grads = scatter_dp(jnp.concatenate([g_w_out_part, g_w_z_part], axis=1))
    g_w_out = early_grads[:, :width_local]
    g_w_z = early_grads[:, width_local:]
    output = tokens + tensor_scatter_rows(branch_part)
    d_xp, d_bc, d_dt, g_cxw, g_cxb, g_cbw, g_cbb, g_alog, g_skip, g_bias = scan_back(d_y)
    x_g = d_xp.astype(jnp.bfloat16)
    after_early = jnp.minimum(jnp.abs(early_grads[0, 0]), 0.0)
    dt_g = (d_dt + after_early).astype(jnp.bfloat16)
    bc_g = d_bc.astype(jnp.bfloat16)
    d_normed_part = dot_nt(gate_g, z_full) + dot_nt(x_g, x_full)
    d_normed_part = d_normed_part + dot_nt(dt_g, dt_full) + dot_nt(bc_g, bc_weight)
    joined = jnp.concatenate([x_g, bc_g, dt_g], axis=1)
    in_grads = scatter_dp(dot_tn(normed, joined))
    g_w_x = in_grads[:, :width_local]
    g_bc_rows = in_grads[:, width_local : width_local + bc_width]
    g_w_dt = in_grads[:, width_local + bc_width :]
    d_normed = tensor_scatter_rows(d_normed_part)
    d_unit_r = d_normed * gain_full[None, :]
    d_tokens = cotangent + inv_rms * (
        d_unit_r - unit_rows * jnp.mean(d_unit_r * unit_rows, axis=1, keepdims=True)
    )

    group_parts = (g_cxw, g_cxb, g_alog, g_skip, g_bias, g_norm_w, g_cbw, g_cbb)
    flat = lax.psum(jnp.concatenate([part.reshape(-1) for part in group_parts]), "dp")
    pieces = []
    offset = 0
    for part in group_parts:
        pieces.append(flat[offset : offset + part.size].reshape(part.shape))
        offset += part.size
    g_cxw, g_cxb, g_alog, g_skip, g_bias, g_norm_w, g_cbw, g_cbb = pieces

    dp_index = lax.axis_index("dp")
    bc_here = lax.dynamic_slice_in_dim(bc_weight, dp_index * weight_rows, weight_rows, 0)
    gain_rows = (
        jnp.sum(g_w_z * w_z.astype(jnp.float32), axis=1)
        + jnp.sum(g_w_x * w_x.astype(jnp.float32), axis=1)
        + jnp.sum(g_w_dt * w_dt.astype(jnp.float32), axis=1)
        + jnp.sum(g_bc_rows * bc_here.astype(jnp.float32), axis=1)
    )
    conv_here = tensor_size * conv_len
    cbw_here = lax.dynamic_slice_in_dim(g_cbw, dp_index * conv_here, conv_here, 0)
    cbb_here = lax.dynamic_slice_in_dim(g_cbb, dp_index * conv_here, conv_here, 0)
    g_w_bc = tensor_scatter_sum(g_bc_rows.reshape(tensor_size, bc_rows, bc_width))
    shared = tensor_scatter_sum(
        jnp.concatenate(
            [
                gain_rows.reshape(tensor_size, gain_len),
                cbw_here.reshape(tensor_size, conv_len * taps),
                cbb_here.reshape(tensor_size, conv_len),
            ],
            axis=1,
        )
    )
    g_gain = shared[:gain_len] / norm_gain
    g_conv_bcw = shared[gain_len : gain_len + conv_len * taps].reshape(conv_len, taps)
    g_conv_bcb = shared[gain_len + conv_len * taps :]
    return (
        output,
        d_tokens,
        g_gain,
        g_w_z,
        g_w_x,
        g_w_dt,
        g_w_bc,
        g_w_out,
        g_cxw,
        g_cxb,
        g_conv_bcw,
        g_conv_bcb,
        g_alog,
        g_skip,
        g_bias,
        g_norm_w,
    )


def solution(mesh):
    return jax.shard_map(
        per_device,
        mesh=mesh,
        in_specs=(
            P(("dp", "tensor"), None),
            P(("dp", "tensor")),
            P("dp", "tensor"),
            P("dp", "tensor"),
            P("dp", "tensor"),
            P(("dp", "tensor"), None),
            P("dp", "tensor"),
            P("tensor", None),
            P("tensor"),
            P(("dp", "tensor"), None),
            P(("dp", "tensor")),
            P("tensor"),
            P("tensor"),
            P("tensor"),
            P("tensor"),
            P("dp"),
            P("dp"),
            P(("dp", "tensor"), None),
        ),
        out_specs=(
            P(("dp", "tensor"), None),
            P(("dp", "tensor"), None),
            P(("dp", "tensor")),
            P("dp", "tensor"),
            P("dp", "tensor"),
            P("dp", "tensor"),
            P(("dp", "tensor"), None),
            P("dp", "tensor"),
            P("tensor", None),
            P("tensor"),
            P(("dp", "tensor"), None),
            P(("dp", "tensor")),
            P("tensor"),
            P("tensor"),
            P("tensor"),
            P("tensor"),
        ),
        check_vma=False,
    )
```
